32 devices in a mesh: tile: 8 (over z, x), grp: 4 (over y, core).
Axes of the slice: x: 2, y: 2, z: 4, core: 2. Of those that a mesh axis runs over, the one named last changes fastest.
Arguments:
- pixels: bfloat16 [8192, 432], P(('tile', 'grp')), may hold values from -25 to 25
- labels: int32 [8192], P(('tile', 'grp')), may hold values from 0 to 63, as said below
- targets: bfloat16 [512, 432], P('grp'), may hold values from -6 to 6
Outputs:
- scores: bfloat16 [8192, 512], P(('tile', 'grp'))
The draws below stay inside these ranges and needn't reach their ends.
Inputs may be any that keep to these rules, and one draw needn't show every extreme that they name: `labels`: among the 256 pixels of each aligned block (rows b * 256 to (b + 1) * 256 - 1) no cluster occurs more than 8 times; in every draw one cluster occurs exactly 8 times in every block.
All inputs are finite; a program needn't handle non-finite values.
Results may differ from the reference program's by a relative error of at most 0.0024.
Values may be sent and summed in bfloat16 or wider, within the bound.
A program may use at most 128 MiB of HBM per device.

```python
import jax
import jax.numpy as jnp
from jax import lax

B = 432
NT = 512
NCLUST = 64
R = 256
CAP = 8
NBLK = 32


def label_table(key):
    keys = jax.random.split(jax.random.fold_in(key, 11), 4)
    common = jax.random.randint(keys[0], (), 0, NCLUST)
    extra = jax.random.randint(keys[1], (NBLK,), 0, NCLUST - 1)
    extra = extra + (extra >= common).astype(jnp.int32)
    slot_cluster = jnp.arange(NCLUST * CAP, dtype=jnp.int32) // CAP
    ranks = jax.vmap(lambda k: jax.random.permutation(k, NCLUST * CAP))(jax.random.split(keys[2], NBLK))
    ranks = ranks.astype(jnp.int32)
    priority = jnp.where(slot_cluster[None, :] == common, -2, jnp.where(slot_cluster[None, :] == extra[:, None], -1, ranks))
    order = jnp.argsort(priority, axis=1, stable=True)[:, :R]
    chosen = (order // CAP).astype(jnp.int32)
    shuffle = jax.vmap(lambda k: jax.random.permutation(k, R))(jax.random.split(keys[3], NBLK))
    chosen = jnp.take_along_axis(chosen, shuffle.astype(jnp.int32), axis=1)
    return chosen.reshape(NBLK * R).astype(jnp.int32)


def draw_labels(key, part):
    return label_table(key)


def draw_pixels(key, part):
    labels = label_table(key)
    keys = jax.random.split(jax.random.fold_in(key, 23), 3)
    means = jax.random.truncated_normal(keys[0], -3.0, 3.0, (NCLUST, B), jnp.float32)
    spread = jnp.exp(jax.random.uniform(keys[1], (NCLUST, B), jnp.float32, jnp.log(0.5), jnp.log(3.0)))
    noise = jax.random.truncated_normal(keys[2], -4.0, 4.0, (NBLK * R, B), jnp.float32)
    padded = jnp.pad(noise, ((0, 0), (1, 1)))
    mixed = noise + 0.4 * (padded[:, 2:] + padded[:, :-2])
    values = means[labels] + spread[labels] * mixed
    return values.astype(jnp.bfloat16)


def steps_of(rng, extent, cuts, least, top_value):
    def one(dim, parts):
        draws = jax.random.uniform(jax.random.fold_in(jax.random.fold_in(rng, 6), dim), (parts,), jnp.float32, least / len(cuts), top_value / len(cuts))
        return jnp.repeat(jnp.exp(draws), extent[dim] // parts).reshape((-1,) + (1,) * (len(extent) - dim - 1))

    loudness = one(*cuts[0])
    for cut in cuts[1:]:
        loudness = loudness * one(*cut)
    return loudness


def scatter_about(stream_key, extent, scale, bound, pieces=(), kind=jnp.bfloat16):
    gain = steps_of(stream_key, extent, pieces, -0.22, 0.18) if pieces else 1.0
    array = jax.random.normal(stream_key, extent, jnp.float32) * scale * gain
    return jnp.minimum(jnp.maximum(array, -bound), bound).astype(kind)


def setup_inputs(seed: int = 0) -> dict:
    splits = jax.random.split(jax.random.key(seed), 4)
    pixels = draw_pixels(jax.random.fold_in(splits[3], 71), 0)
    labels = draw_labels(jax.random.fold_in(splits[3], 71), 0)
    targets = scatter_about(splits[2], (NT, B), 1.0, 6.0, ((0, 4),))
    return {"pixels": pixels, "labels": labels, "targets": targets}


def slot_numbers(lab_block):
    clusters = jnp.arange(NCLUST, dtype=jnp.int32)
    member = (lab_block[:, None] == clusters[None, :]).astype(jnp.int32)
    place_rank = jnp.sum(jnp.cumsum(member, axis=0) * member, axis=1) - 1
    return (lab_block * CAP + place_rank).astype(jnp.int32)

def group_block(pix_block, lab_block):
    slot_index = slot_numbers(lab_block)
    table = jnp.zeros((NCLUST * CAP, B), pix_block.dtype).at[slot_index].set(pix_block)
    return (table.reshape(NCLUST, CAP, B), slot_index)

def reference(pixels, labels, targets):
    block_count = pixels.shape[0] // R
    pix_blocks = pixels.reshape(block_count, R, B)
    lab_blocks = labels.reshape(block_count, R)

    def accumulate(running, block_item):
        grouped, slot_index = group_block(block_item[0], block_item[1])
        gram_part = jnp.einsum('cwb,cwd->cbd', grouped.astype(jnp.float32), grouped.astype(jnp.float32), preferred_element_type=jnp.float32)
        sum_part = jnp.sum(grouped, axis=1, dtype=jnp.float32)
        return ((running[0] + gram_part, running[1] + sum_part), None)
    start_state = (jnp.zeros((NCLUST, B, B), jnp.float32), jnp.zeros((NCLUST, B), jnp.float32))
    (gram_sum, first_sums), _ = lax.scan(accumulate, start_state, (pix_blocks, lab_blocks))
    clusters = jnp.arange(NCLUST, dtype=jnp.int32)
    counts = jnp.sum((labels[:, None] == clusters[None, :]).astype(jnp.float32), axis=0)
    counts = jnp.maximum(counts, 1.0)
    centre = first_sums / counts[:, None]
    identity = jnp.eye(B, dtype=jnp.float32)
    covariance = gram_sum / counts[:, None, None] - centre[:, :, None] * centre[:, None, :] + 0.05 * identity
    factor = jnp.linalg.cholesky(covariance)
    inverse = jax.scipy.linalg.solve_triangular(factor, jnp.broadcast_to(identity, factor.shape), lower=True)
    whitened = jnp.einsum('tb,cdb->ctd', targets.astype(jnp.float32), inverse, precision=lax.Precision.HIGHEST)
    lib_norm = jnp.sum(whitened * whitened, axis=-1)

    def score_block(block_item):
        grouped, slot_index = group_block(block_item[0], block_item[1])
        centered = grouped.astype(jnp.float32) - centre[:, None, :]
        white_pix = jnp.einsum('cwb,cdb->cwd', centered, inverse, precision=lax.Precision.HIGHEST)
        inner_prod = jnp.einsum('cwd,ctd->cwt', white_pix, whitened, precision=lax.Precision.HIGHEST)
        pix_norm = jnp.sum(white_pix * white_pix, axis=-1)
        result = B * inner_prod * inner_prod / ((lib_norm[:, None, :] + 1e-06) * (pix_norm[:, :, None] + 1e-06))
        result = result.astype(jnp.bfloat16).reshape(NCLUST * CAP, NT)
        return result[slot_index]
    scores = lax.map(score_block, (pix_blocks, lab_blocks))
    return scores.reshape(block_count * R, NT)
```

```python
import functools

import jax
import jax.numpy as jnp
from jax import lax
from jax.experimental import pallas as pl
from jax.experimental.pallas import tpu as pltpu
from jax.sharding import PartitionSpec as P

NCLUST = 64
CAP = 8
RIDGE = 0.05
LIFT = 1.0
EPS = 1e-06
STEP = 32
LANES = 128
AXES = ("tile", "grp")
HI = lax.Precision.HIGHEST
F32 = jnp.float32
BF16 = jnp.bfloat16


def dot_t(a, b, prec=None):
    return lax.dot_general(a, b, (((1,), (1,)), ((), ())), precision=prec, preferred_element_type=F32)


def dot_0(a, b, prec=None):
    return lax.dot_general(a, b, (((0,), (0,)), ((), ())), precision=prec, preferred_element_type=F32)


def dot_n(a, b, prec=None):
    return lax.dot_general(a, b, (((1,), (0,)), ((), ())), precision=prec, preferred_element_type=F32)


def panel_inverse(panels, first):
    rows, width = panels[0].shape
    lane = lax.broadcasted_iota(jnp.int32, (rows, width), 1)
    row = lax.broadcasted_iota(jnp.int32, (rows, width), 0)
    lane1 = lax.broadcasted_iota(jnp.int32, (1, width), 1)
    for j in range(rows):
        at = first + j
        fresh = []
        for panel in panels:
            col = panel[:, at : at + 1]
            inv = 1.0 / col[j : j + 1, :]
            norm = jnp.where(lane1 == at, 1.0, panel[j : j + 1, :]) * inv
            rest = jnp.where(lane == at, 0.0, panel) - col * norm
            fresh.append(jnp.where(row == j, norm, rest))
        panels = fresh
    return panels


def invert_all(mats):
    size = mats[0].shape[0]
    lane1 = lax.broadcasted_iota(jnp.int32, (1, size), 1)
    for k in range(size // STEP):
        lo = k * STEP
        inside = (lane1 >= lo) & (lane1 < lo + STEP)
        sign = jnp.where(lane1 < lo, -1.0, jnp.where(inside, 0.0, 1.0))
        rows = [m[lo : lo + STEP, :] for m in mats]
        outs = panel_inverse(rows, lo)
        fresh = []
        for m, r, w in zip(mats, rows, outs):
            kept = jnp.where(inside, 0.0, m)
            upd = kept - dot_0(r * sign, w, HI)
            parts = [upd[:lo]] * (lo > 0) + [w] + [upd[lo + STEP :]] * (lo + STEP < size)
            fresh.append(jnp.concatenate(parts, axis=0))
        mats = fresh
    return mats


def cluster_gram(x, bands):
    size = x.shape[0]
    gram = dot_t(x, x)
    valid = x[:, bands : bands + 1].astype(F32)
    ri = lax.broadcasted_iota(jnp.int32, (size, size), 0)
    ci = lax.broadcasted_iota(jnp.int32, (size, size), 1)
    diag = ri == ci
    valid_row = jnp.sum(jnp.where(diag, valid, 0.0), axis=0, keepdims=True)
    count = jnp.maximum(jnp.sum(valid), 1.0)
    share = 1.0 / count
    mean_r = jnp.sum(gram, axis=0, keepdims=True) * share
    mean_c = jnp.sum(gram, axis=1, keepdims=True) * share
    mean = jnp.sum(mean_r) * share
    mat = (gram - mean_r - mean_c + (mean + LIFT)) * (valid * valid_row) * share
    mat = mat + jnp.where(diag, RIDGE, 0.0)
    return mat, valid, count, diag


def cluster_scores(x, targets, tnorm, inverse, valid, count, diag, bands):
    share = 1.0 / count
    u = dot_t(x, targets)
    u = (u - jnp.sum(u, axis=0, keepdims=True) * share) * valid
    z = dot_n(inverse, u, HI)
    kd = jnp.sum(jnp.where(diag, inverse, 0.0), axis=1, keepdims=True)
    pix = count * (1.0 - RIDGE * kd) - LIFT / (LIFT + RIDGE)
    pix = jnp.maximum(pix, 0.0) + EPS
    lib = (tnorm - jnp.sum(u * z, axis=0, keepdims=True) * share) * (1.0 / RIDGE)
    lib = jnp.maximum(lib, 0.0) + EPS
    return z * z * (bands / pix) * (1.0 / lib)


def owner_body(bands, owned, x_ref, t_ref, out_ref):
    slots = x_ref.shape[0]
    devices = slots // (owned * CAP)
    width = x_ref.shape[1]
    xf = x_ref[...].astype(F32).reshape(devices, owned, CAP, width)
    xs = [xf[:, c].reshape(devices * CAP, width).astype(BF16) for c in range(owned)]
    grams = [cluster_gram(x, bands) for x in xs]
    inverses = invert_all([g[0] for g in grams])
    targets = t_ref[...]
    tf = targets.astype(F32)
    tnorm = dot_t(jnp.ones((8, width), F32), tf * tf, HI)[0:1]
    res = []
    for x, g, inv in zip(xs, grams, inverses):
        s = cluster_scores(x, targets, tnorm, inv, g[1], g[2], g[3], bands)
        res.append(s.reshape(devices, 1, CAP, s.shape[1]))
    full = jnp.concatenate(res, axis=1)
    out_ref[...] = full.reshape(slots, full.shape[-1]).astype(BF16)


def narrow(pixels, labels, targets):
    devices = lax.axis_size("tile") * lax.axis_size("grp")
    owned = NCLUST // devices
    bands = pixels.shape[1]
    width = -(-(bands + 1) // LANES) * LANES
    slots = NCLUST * CAP
    clusters = jnp.arange(NCLUST, dtype=jnp.int32)
    member = (labels[:, None] == clusters[None, :]).astype(jnp.int32)
    rank = jnp.sum(jnp.cumsum(member, axis=0) * member, axis=1) - 1
    index = labels * CAP + rank
    onehot = (index[:, None] == jnp.arange(slots, dtype=jnp.int32)[None, :]).astype(BF16)
    ones = jnp.ones((pixels.shape[0], 1), BF16)
    wide = jnp.concatenate([pixels, ones, jnp.zeros((pixels.shape[0], width - bands - 1), BF16)], axis=1)
    outgoing = dot_0(onehot, wide).astype(BF16)
    arrived = lax.all_to_all(outgoing, AXES, split_axis=0, concat_axis=0, tiled=True)
    library = lax.all_gather(targets, "grp", axis=0, tiled=True)
    library = jnp.pad(library, ((0, 0), (0, width - bands)))
    out = pl.pallas_call(
        functools.partial(owner_body, bands, owned),
        out_shape=jax.ShapeDtypeStruct((slots, library.shape[0]), BF16),
        in_specs=[pl.BlockSpec(memory_space=pltpu.VMEM)] * 2,
        out_specs=pl.BlockSpec(memory_space=pltpu.VMEM),
        compiler_params=pltpu.CompilerParams(vmem_limit_bytes=60 * 1024 * 1024),
    )(arrived, library)
    returned = lax.all_to_all(out, AXES, split_axis=0, concat_axis=0, tiled=True)
    return dot_n(onehot, returned).astype(BF16)


def wide_cluster(pixels, labels, targets):
    n_tile = lax.axis_size("tile")
    n_grp = lax.axis_size("grp")
    band_count = pixels.shape[1]
    per_owner = 2 * NCLUST // n_tile
    target_total = targets.shape[0] * n_grp
    clusters = jnp.arange(NCLUST, dtype=jnp.int32)
    member = (labels[:, None] == clusters[None, :]).astype(jnp.int32)
    local_count = jnp.sum(member, axis=0).astype(jnp.float32)
    counts = lax.psum(local_count, ("tile", "grp"))
    place_rank = jnp.sum(jnp.cumsum(member, axis=0) * member, axis=1) - 1
    owner_pair = labels // per_owner
    inner_slot = labels % per_owner
    slot_width = CAP
    target_tile = 2 * owner_pair
    slot_index = (target_tile * per_owner + inner_slot) * slot_width + place_rank
    slot_total = n_tile * per_owner * slot_width
    outgoing = jnp.zeros((slot_total, band_count), jnp.bfloat16).at[slot_index].set(pixels)
    outgoing = outgoing.reshape(n_tile, per_owner * slot_width, band_count)
    arrived = lax.all_to_all(outgoing, "tile", split_axis=0, concat_axis=0, tiled=True)
    grouped = arrived.reshape(n_tile, per_owner, slot_width, band_count)
    gram_sum = jnp.einsum("scwb,scwd->cbd", grouped, grouped, preferred_element_type=jnp.float32)
    first_sums = jnp.sum(grouped, axis=(0, 2), dtype=jnp.float32)
    gram_sum, first_sums = lax.psum((gram_sum, first_sums), "grp")
    own_pair = lax.axis_index("tile") // 2
    own_counts = lax.dynamic_slice_in_dim(counts, own_pair * per_owner, per_owner, 0)
    own_counts = jnp.maximum(own_counts, 1.0)
    centre = first_sums / own_counts[:, None]
    identity = jnp.eye(band_count, dtype=jnp.float32)
    covariance = (
        gram_sum / own_counts[:, None, None]
        - centre[:, :, None] * centre[:, None, :]
        + 0.05 * identity
    )
    factor = jnp.linalg.cholesky(covariance)
    inverse = jax.scipy.linalg.solve_triangular(
        factor, jnp.broadcast_to(identity, factor.shape), lower=True
    )
    whitened = jnp.einsum(
        "tb,cdb->ctd",
        lax.all_gather(targets, "grp", axis=0, tiled=True).astype(jnp.float32),
        inverse,
        precision=lax.Precision.HIGHEST,
    )
    lib_norm = jnp.sum(whitened * whitened, axis=-1)
    centered = grouped.astype(jnp.float32) - centre[None, :, None, :]
    white_pix = jnp.einsum("scwb,cdb->scwd", centered, inverse, precision=lax.Precision.HIGHEST)
    inner_prod = jnp.einsum("scwd,ctd->scwt", white_pix, whitened, precision=lax.Precision.HIGHEST)
    pix_norm = jnp.sum(white_pix * white_pix, axis=-1)
    result = (
        band_count
        * inner_prod
        * inner_prod
        / ((lib_norm[None, :, None, :] + 1e-06) * (pix_norm[:, :, :, None] + 1e-06))
    )
    outbound = result.astype(jnp.bfloat16).reshape(n_tile, per_owner * slot_width, target_total)
    returned = lax.all_to_all(outbound, "tile", split_axis=0, concat_axis=0, tiled=True)
    flat_scores = returned.reshape(slot_total, target_total)
    return flat_scores[slot_index]


def local(pixels, labels, targets):
    devices = lax.axis_size("tile") * lax.axis_size("grp")
    if NCLUST % devices == 0 and devices * CAP <= pixels.shape[1]:
        return narrow(pixels, labels, targets)
    return wide_cluster(pixels, labels, targets)


def solution(mesh):
    return jax.shard_map(
        local,
        mesh=mesh,
        in_specs=(P(("tile", "grp"), None), P(("tile", "grp")), P("grp", None)),
        out_specs=P(("tile", "grp"), None),
        check_vma=False,
    )
```

```python
import functools

import jax
import jax.numpy as jnp
from jax import lax
from jax.experimental import pallas as pl
from jax.experimental.pallas import tpu as pltpu
from jax.sharding import PartitionSpec as P

NCLUST = 64
CAP = 8
RIDGE = 0.05
LIFT = 1.0
EPS = 1e-06
STEP = 32
LANES = 128
MESH = pl.DeviceIdType.MESH
HI = lax.Precision.HIGHEST
F32 = jnp.float32
BF16 = jnp.bfloat16


def dot_t(a, b, prec=None):
    return lax.dot_general(a, b, (((1,), (1,)), ((), ())), precision=prec, preferred_element_type=F32)


def dot_0(a, b, prec=None):
    return lax.dot_general(a, b, (((0,), (0,)), ((), ())), precision=prec, preferred_element_type=F32)


def dot_n(a, b, prec=None):
    return lax.dot_general(a, b, (((1,), (0,)), ((), ())), precision=prec, preferred_element_type=F32)


def panel_inverse(panels, first):
    rows, width = panels[0].shape
    lane = lax.broadcasted_iota(jnp.int32, (rows, width), 1)
    row = lax.broadcasted_iota(jnp.int32, (rows, width), 0)
    lane1 = lax.broadcasted_iota(jnp.int32, (1, width), 1)
    for j in range(rows):
        at = first + j
        fresh = []
        for panel in panels:
            col = panel[:, at : at + 1]
            inv = 1.0 / col[j : j + 1, :]
            norm = jnp.where(lane1 == at, 1.0, panel[j : j + 1, :]) * inv
            rest = jnp.where(lane == at, 0.0, panel) - col * norm
            fresh.append(jnp.where(row == j, norm, rest))
        panels = fresh
    return panels


def invert_all(mats):
    size = mats[0].shape[0]
    lane1 = lax.broadcasted_iota(jnp.int32, (1, size), 1)
    for k in range(size // STEP):
        lo = k * STEP
        inside = (lane1 >= lo) & (lane1 < lo + STEP)
        sign = jnp.where(lane1 < lo, -1.0, jnp.where(inside, 0.0, 1.0))
        rows = [m[lo : lo + STEP, :] for m in mats]
        outs = panel_inverse(rows, lo)
        fresh = []
        for m, r, w in zip(mats, rows, outs):
            kept = jnp.where(inside, 0.0, m)
            upd = kept - dot_0(r * sign, w, HI)
            parts = [upd[:lo]] * (lo > 0) + [w] + [upd[lo + STEP :]] * (lo + STEP < size)
            fresh.append(jnp.concatenate(parts, axis=0))
        mats = fresh
    return mats


def cluster_gram(x, bands):
    size = x.shape[0]
    gram = dot_t(x, x)
    valid = x[:, bands : bands + 1].astype(F32)
    ri = lax.broadcasted_iota(jnp.int32, (size, size), 0)
    ci = lax.broadcasted_iota(jnp.int32, (size, size), 1)
    diag = ri == ci
    valid_row = jnp.sum(jnp.where(diag, valid, 0.0), axis=0, keepdims=True)
    count = jnp.maximum(jnp.sum(valid), 1.0)
    share = 1.0 / count
    mean_r = jnp.sum(gram, axis=0, keepdims=True) * share
    mean_c = jnp.sum(gram, axis=1, keepdims=True) * share
    mean = jnp.sum(mean_r) * share
    mat = (gram - mean_r - mean_c + (mean + LIFT)) * (valid * valid_row) * share
    mat = mat + jnp.where(diag, RIDGE, 0.0)
    return mat, valid, count, diag


def cluster_scores(x, targets, tnorm, inverse, valid, count, diag, bands):
    share = 1.0 / count
    u = dot_t(x, targets)
    u = (u - jnp.sum(u, axis=0, keepdims=True) * share) * valid
    z = dot_n(inverse, u, HI)
    kd = jnp.sum(jnp.where(diag, inverse, 0.0), axis=1, keepdims=True)
    pix = count * (1.0 - RIDGE * kd) - LIFT / (LIFT + RIDGE)
    pix = jnp.maximum(pix, 0.0) + EPS
    lib = (tnorm - jnp.sum(u * z, axis=0, keepdims=True) * share) * (1.0 / RIDGE)
    lib = jnp.maximum(lib, 0.0) + EPS
    return z * z * (bands / pix) * (1.0 / lib)


def slot_of(lab_row, slots):
    count = lab_row.shape[1]
    ri = lax.broadcasted_iota(jnp.int32, (count, count), 0)
    ci = lax.broadcasted_iota(jnp.int32, (count, count), 1)
    lab_row = lab_row.astype(F32)
    lab_col = jnp.sum(jnp.where(ri == ci, lab_row, 0.0), axis=1, keepdims=True)
    same = jnp.where(lab_row == lab_col, 1.0, 0.0)
    rank_col = jnp.sum(jnp.where(ci < ri, same, 0.0), axis=1, keepdims=True)
    rank_row = jnp.sum(jnp.where(ri < ci, same, 0.0), axis=0, keepdims=True)
    idx_col = lab_col * CAP + rank_col
    idx_row = lab_row * CAP + rank_row
    across = lax.broadcasted_iota(jnp.int32, (count, slots), 1).astype(F32)
    down = lax.broadcasted_iota(jnp.int32, (slots, count), 0).astype(F32)
    take = jnp.where(across == idx_col, 1.0, 0.0).astype(BF16)
    put = jnp.where(down == idx_row, 1.0, 0.0).astype(BF16)
    return take, put


def step_body(
    bands, owned, n_tile, n_grp,
    lab_ref, pix_ref, tgt_ref, out_ref,
    wide, outgoing, arrived, mine, library, outbound, returned, take_ref,
    send_a, recv_a, send_t, recv_t, send_b, recv_b,
):
    devices = n_tile * n_grp
    group = owned * CAP
    slots = devices * group
    width = wide.shape[1]
    tile = lax.axis_index("tile")
    grp = lax.axis_index("grp")
    me = tile * n_grp + grp

    def place(r):
        other = lax.rem(me + r, devices)
        return (lax.div(other, n_grp), lax.rem(other, n_grp)), other

    barrier = pltpu.get_barrier_semaphore()

    def greet(r, _):
        pl.semaphore_signal(barrier, inc=1, device_id=place(r)[0], device_id_type=MESH)
        return 0

    lax.fori_loop(1, devices, greet, 0)

    wide[...] = jnp.ones_like(wide)
    wide[:, :bands] = pix_ref[...]
    mine[...] = jnp.zeros_like(mine)
    mine[:, :bands] = tgt_ref[...]
    take, put = slot_of(lab_ref[...], slots)
    take_ref[...] = take
    outgoing[...] = dot_n(put, wide[...]).astype(BF16).reshape(devices, group, width)
    pl.semaphore_wait(barrier, devices - 1)

    def ship(src, dst, sends, recvs, r):
        where, other = place(r)
        return pltpu.make_async_remote_copy(
            src_ref=src.at[other], dst_ref=dst.at[me],
            send_sem=sends.at[r], recv_sem=recvs.at[r],
            device_id=where, device_id_type=MESH,
        )

    def lend(r):
        return pltpu.make_async_remote_copy(
            src_ref=mine, dst_ref=library.at[grp],
            send_sem=send_t.at[r], recv_sem=recv_t.at[r],
            device_id=(tile, lax.rem(grp + r, n_grp)), device_id_type=MESH,
        )

    def start_a(r, _):
        ship(outgoing, arrived, send_a, recv_a, r).start()
        return 0

    def wait_a(r, _):
        ship(outgoing, arrived, send_a, recv_a, r).wait()
        return 0

    def start_b(r, _):
        ship(outbound, returned, send_b, recv_b, r).start()
        return 0

    def wait_b(r, _):
        ship(outbound, returned, send_b, recv_b, r).wait()
        return 0

    lax.fori_loop(1, devices, start_a, 0)
    for r in range(1, n_grp):
        lend(r).start()
    arrived[me] = outgoing[me]
    library[grp] = mine[...]
    lax.fori_loop(1, devices, wait_a, 0)

    xf = arrived[...].astype(F32).reshape(devices, owned, CAP, width)
    xs = [xf[:, c].reshape(devices * CAP, width).astype(BF16) for c in range(owned)]
    grams = [cluster_gram(x, bands) for x in xs]
    inverses = invert_all([g[0] for g in grams])
    for r in range(1, n_grp):
        lend(r).wait()
    targets = library[...].reshape(n_grp * mine.shape[0], width)
    tf = targets.astype(F32)
    tnorm = dot_t(jnp.ones((8, width), F32), tf * tf, HI)[0:1]
    res = []
    for x, g, inv in zip(xs, grams, inverses):
        s = cluster_scores(x, targets, tnorm, inv, g[1], g[2], g[3], bands)
        res.append(s.reshape(devices, 1, CAP, s.shape[1]))
    full = jnp.concatenate(res, axis=1).reshape(devices, group, targets.shape[0])
    outbound[...] = full.astype(BF16)
    lax.fori_loop(1, devices, start_b, 0)
    returned[me] = outbound[me]
    lax.fori_loop(1, devices, wait_b, 0)
    out_ref[...] = dot_n(take_ref[...], returned[...].reshape(slots, targets.shape[0])).astype(BF16)


def narrow(pixels, labels, targets):
    n_tile, n_grp = lax.axis_size("tile"), lax.axis_size("grp")
    devices = n_tile * n_grp
    owned = NCLUST // devices
    group = owned * CAP
    rows, bands = pixels.shape
    width = -(-(bands + 1) // LANES) * LANES
    total = targets.shape[0] * n_grp
    vmem = pl.BlockSpec(memory_space=pltpu.VMEM)
    dma = pltpu.SemaphoreType.DMA
    return pl.pallas_call(
        functools.partial(step_body, bands, owned, n_tile, n_grp),
        out_shape=jax.ShapeDtypeStruct((rows, total), BF16),
        in_specs=[vmem] * 3,
        out_specs=vmem,
        scratch_shapes=[
            pltpu.VMEM((rows, width), BF16),
            pltpu.VMEM((devices, group, width), BF16),
            pltpu.VMEM((devices, group, width), BF16),
            pltpu.VMEM((targets.shape[0], width), BF16),
            pltpu.VMEM((n_grp, targets.shape[0], width), BF16),
            pltpu.VMEM((devices, group, total), BF16),
            pltpu.VMEM((devices, group, total), BF16),
            pltpu.VMEM((rows, NCLUST * CAP), BF16),
            dma((devices,)), dma((devices,)),
            dma((n_grp,)), dma((n_grp,)),
            dma((devices,)), dma((devices,)),
        ],
        compiler_params=pltpu.CompilerParams(
            collective_id=0, has_side_effects=True, vmem_limit_bytes=60 * 1024 * 1024
        ),
    )(labels.reshape(1, rows), pixels, targets)


def wide_cluster(pixels, labels, targets):
    n_tile = lax.axis_size("tile")
    n_grp = lax.axis_size("grp")
    band_count = pixels.shape[1]
    per_owner = 2 * NCLUST // n_tile
    target_total = targets.shape[0] * n_grp
    clusters = jnp.arange(NCLUST, dtype=jnp.int32)
    member = (labels[:, None] == clusters[None, :]).astype(jnp.int32)
    local_count = jnp.sum(member, axis=0).astype(jnp.float32)
    counts = lax.psum(local_count, ("tile", "grp"))
    place_rank = jnp.sum(jnp.cumsum(member, axis=0) * member, axis=1) - 1
    owner_pair = labels // per_owner
    inner_slot = labels % per_owner
    slot_width = CAP
    target_tile = 2 * owner_pair
    slot_index = (target_tile * per_owner + inner_slot) * slot_width + place_rank
    slot_total = n_tile * per_owner * slot_width
    outgoing = jnp.zeros((slot_total, band_count), jnp.bfloat16).at[slot_index].set(pixels)
    outgoing = outgoing.reshape(n_tile, per_owner * slot_width, band_count)
    arrived = lax.all_to_all(outgoing, "tile", split_axis=0, concat_axis=0, tiled=True)
    grouped = arrived.reshape(n_tile, per_owner, slot_width, band_count)
    gram_sum = jnp.einsum("scwb,scwd->cbd", grouped, grouped, preferred_element_type=jnp.float32)
    first_sums = jnp.sum(grouped, axis=(0, 2), dtype=jnp.float32)
    gram_sum, first_sums = lax.psum((gram_sum, first_sums), "grp")
    own_pair = lax.axis_index("tile") // 2
    own_counts = lax.dynamic_slice_in_dim(counts, own_pair * per_owner, per_owner, 0)
    own_counts = jnp.maximum(own_counts, 1.0)
    centre = first_sums / own_counts[:, None]
    identity = jnp.eye(band_count, dtype=jnp.float32)
    covariance = (
        gram_sum / own_counts[:, None, None]
        - centre[:, :, None] * centre[:, None, :]
        + 0.05 * identity
    )
    factor = jnp.linalg.cholesky(covariance)
    inverse = jax.scipy.linalg.solve_triangular(
        factor, jnp.broadcast_to(identity, factor.shape), lower=True
    )
    whitened = jnp.einsum(
        "tb,cdb->ctd",
        lax.all_gather(targets, "grp", axis=0, tiled=True).astype(jnp.float32),
        inverse,
        precision=lax.Precision.HIGHEST,
    )
    lib_norm = jnp.sum(whitened * whitened, axis=-1)
    centered = grouped.astype(jnp.float32) - centre[None, :, None, :]
    white_pix = jnp.einsum("scwb,cdb->scwd", centered, inverse, precision=lax.Precision.HIGHEST)
    inner_prod = jnp.einsum("scwd,ctd->scwt", white_pix, whitened, precision=lax.Precision.HIGHEST)
    pix_norm = jnp.sum(white_pix * white_pix, axis=-1)
    result = (
        band_count
        * inner_prod
        * inner_prod
        / ((lib_norm[None, :, None, :] + 1e-06) * (pix_norm[:, :, :, None] + 1e-06))
    )
    outbound = result.astype(jnp.bfloat16).reshape(n_tile, per_owner * slot_width, target_total)
    returned = lax.all_to_all(outbound, "tile", split_axis=0, concat_axis=0, tiled=True)
    flat_scores = returned.reshape(slot_total, target_total)
    return flat_scores[slot_index]


def local(pixels, labels, targets):
    devices = lax.axis_size("tile") * lax.axis_size("grp")
    if NCLUST % devices == 0 and devices * CAP <= pixels.shape[1]:
        return narrow(pixels, labels, targets)
    return wide_cluster(pixels, labels, targets)


def solution(mesh):
    return jax.shard_map(
        local,
        mesh=mesh,
        in_specs=(P(("tile", "grp"), None), P(("tile", "grp")), P("grp", None)),
        out_specs=P(("tile", "grp"), None),
        check_vma=False,
    )
```

```python
import functools

import jax
import jax.numpy as jnp
from jax import lax
from jax.experimental import pallas as pl
from jax.experimental.pallas import tpu as pltpu
from jax.sharding import PartitionSpec as P

NCLUST = 64
CAP = 8
RIDGE = 0.05
LIFT = 1.0
EPS = 1e-06
STEP = 64
LANES = 128
SUB = 8
PIV = 4
MESH = pl.DeviceIdType.MESH
HI = lax.Precision.HIGHEST
F32 = jnp.float32
BF16 = jnp.bfloat16


def dot_t(a, b, prec=None):
    return lax.dot_general(a, b, (((1,), (1,)), ((), ())), precision=prec, preferred_element_type=F32)


def dot_0(a, b, prec=None):
    return lax.dot_general(a, b, (((0,), (0,)), ((), ())), precision=prec, preferred_element_type=F32)


def dot_n(a, b, prec=None):
    return lax.dot_general(a, b, (((1,), (0,)), ((), ())), precision=prec, preferred_element_type=F32)


def pivot_inverse(e):
    r = 1.0 / (e[0][0] * e[1][1] - e[0][1] * e[0][1])
    i00, i01, i11 = e[1][1] * r, -e[0][1] * r, e[0][0] * r
    x00 = i00 * e[0][2] + i01 * e[1][2]
    x01 = i00 * e[0][3] + i01 * e[1][3]
    x10 = i01 * e[0][2] + i11 * e[1][2]
    x11 = i01 * e[0][3] + i11 * e[1][3]
    s00 = e[2][2] - (e[0][2] * x00 + e[1][2] * x10)
    s01 = e[2][3] - (e[0][2] * x01 + e[1][2] * x11)
    s11 = e[3][3] - (e[0][3] * x01 + e[1][3] * x11)
    q = 1.0 / (s00 * s11 - s01 * s01)
    t00, t01, t11 = s11 * q, -s01 * q, s00 * q
    y00 = -(x00 * t00 + x01 * t01)
    y01 = -(x00 * t01 + x01 * t11)
    y10 = -(x10 * t00 + x11 * t01)
    y11 = -(x10 * t01 + x11 * t11)
    n00 = i00 - (y00 * x00 + y01 * x01)
    n01 = i01 - (y00 * x10 + y01 * x11)
    n11 = i11 - (y10 * x10 + y11 * x11)
    return [[n00, n01, y00, y01], [n01, n11, y10, y11], [y00, y10, t00, t01], [y01, y11, t01, t11]]


def panel_step(tiles, first, j):
    rows = tiles[0].shape[0]
    at = first + j
    home, off = at // LANES, at % LANES
    group = j // SUB * SUB
    lane8 = lax.broadcasted_iota(jnp.int32, (SUB, LANES), 1)
    lanes = lax.broadcasted_iota(jnp.int32, (rows, LANES), 1)
    sub8 = lax.broadcasted_iota(jnp.int32, (SUB, LANES), 0)
    cols = [jnp.broadcast_to(tiles[home][:, off + c : off + c + 1], (rows, LANES)) for c in range(PIV)]
    spread = lambda v, a: jnp.broadcast_to(v[j + a : j + a + 1, :], (SUB, LANES))
    inv = pivot_inverse([[spread(cols[c], a) for c in range(PIV)] for a in range(PIV)])
    fresh = []
    for t, tile in enumerate(tiles):
        src = [spread(tile, c) for c in range(PIV)]
        kept = tile
        if t == home:
            block = (lane8 >= off) & (lane8 < off + PIV)
            src = [jnp.where(block, jnp.where(lane8 == off + c, 1.0, 0.0), v) for c, v in enumerate(src)]
            kept = jnp.where((lanes >= off) & (lanes < off + PIV), 0.0, tile)
        norm = [(inv[a][0] * src[0] + inv[a][1] * src[1]) + (inv[a][2] * src[2] + inv[a][3] * src[3]) for a in range(PIV)]
        wide = [jnp.concatenate([v] * (rows // SUB), axis=0) for v in norm]
        rest = kept - ((cols[0] * wide[0] + cols[1] * wide[1]) + (cols[2] * wide[2] + cols[3] * wide[3]))
        own = rest[group : group + SUB]
        for a in range(PIV):
            own = jnp.where(sub8 == j - group + a, norm[a], own)
        parts = [rest[:group]] * (group > 0) + [own] + [rest[group + SUB :]] * (group + SUB < rows)
        fresh.append(jnp.concatenate(parts, axis=0) if len(parts) > 1 else parts[0])
    return fresh


def panel_inverse(panels, first):
    rows, width = panels[0].shape
    split = [[p[:, t : t + LANES] for t in range(0, width, LANES)] for p in panels]
    for j in range(0, rows, PIV):
        split = [panel_step(tiles, first, j) for tiles in split]
    return [jnp.concatenate(tiles, axis=1) for tiles in split]


def invert_all(mats):
    size = mats[0].shape[0]
    lane1 = lax.broadcasted_iota(jnp.int32, (1, size), 1)
    for k in range(size // STEP):
        lo = k * STEP
        inside = (lane1 >= lo) & (lane1 < lo + STEP)
        sign = jnp.where(lane1 < lo, -1.0, jnp.where(inside, 0.0, 1.0))
        rows = [m[lo : lo + STEP, :] for m in mats]
        outs = panel_inverse(rows, lo)
        fresh = []
        for m, r, w in zip(mats, rows, outs):
            kept = jnp.where(inside, 0.0, m)
            upd = kept - dot_0(r * sign, w, HI)
            parts = [upd[:lo]] * (lo > 0) + [w] + [upd[lo + STEP :]] * (lo + STEP < size)
            fresh.append(jnp.concatenate(parts, axis=0))
        mats = fresh
    return mats


def cluster_gram(x, bands):
    size = x.shape[0]
    gram = dot_t(x, x)
    valid = x[:, bands : bands + 1].astype(F32)
    ri = lax.broadcasted_iota(jnp.int32, (size, size), 0)
    ci = lax.broadcasted_iota(jnp.int32, (size, size), 1)
    diag = ri == ci
    valid_row = jnp.sum(jnp.where(diag, valid, 0.0), axis=0, keepdims=True)
    count = jnp.maximum(jnp.sum(valid), 1.0)
    share = 1.0 / count
    mean_r = jnp.sum(gram, axis=0, keepdims=True) * share
    mean_c = jnp.sum(gram, axis=1, keepdims=True) * share
    mean = jnp.sum(mean_r) * share
    mat = (gram - mean_r - mean_c + (mean + LIFT)) * (valid * valid_row) * share
    mat = mat + jnp.where(diag, RIDGE, 0.0)
    return mat, valid, count, diag


def cluster_scores(x, targets, tnorm, inverse, valid, count, diag, bands):
    share = 1.0 / count
    u = dot_t(x, targets)
    u = (u - jnp.sum(u, axis=0, keepdims=True) * share) * valid
    z = dot_n(inverse, u, HI)
    kd = jnp.sum(jnp.where(diag, inverse, 0.0), axis=1, keepdims=True)
    pix = count * (1.0 - RIDGE * kd) - LIFT / (LIFT + RIDGE)
    pix = jnp.maximum(pix, 0.0) + EPS
    lib = (tnorm - jnp.sum(u * z, axis=0, keepdims=True) * share) * (1.0 / RIDGE)
    lib = jnp.maximum(lib, 0.0) + EPS
    return z * z * (bands / pix) * (1.0 / lib)


def slot_of(lab_row, slots):
    count = lab_row.shape[1]
    ri = lax.broadcasted_iota(jnp.int32, (count, count), 0)
    ci = lax.broadcasted_iota(jnp.int32, (count, count), 1)
    lab_row = lab_row.astype(F32)
    lab_col = jnp.sum(jnp.where(ri == ci, lab_row, 0.0), axis=1, keepdims=True)
    same = jnp.where(lab_row == lab_col, 1.0, 0.0)
    rank_col = jnp.sum(jnp.where(ci < ri, same, 0.0), axis=1, keepdims=True)
    rank_row = jnp.sum(jnp.where(ri < ci, same, 0.0), axis=0, keepdims=True)
    idx_col = lab_col * CAP + rank_col
    idx_row = lab_row * CAP + rank_row
    across = lax.broadcasted_iota(jnp.int32, (count, slots), 1).astype(F32)
    down = lax.broadcasted_iota(jnp.int32, (slots, count), 0).astype(F32)
    take = jnp.where(across == idx_col, 1.0, 0.0).astype(BF16)
    put = jnp.where(down == idx_row, 1.0, 0.0).astype(BF16)
    return take, put


def step_body(
    bands, owned, n_tile, n_grp,
    lab_ref, pix_ref, tgt_ref, out_ref,
    wide, outgoing, arrived, mine, library, outbound, returned, take_ref,
    send_a, recv_a, send_t, recv_t, send_b, recv_b,
):
    devices = n_tile * n_grp
    group = owned * CAP
    slots = devices * group
    width = wide.shape[1]
    tile = lax.axis_index("tile")
    grp = lax.axis_index("grp")
    me = tile * n_grp + grp

    def place(r):
        other = lax.rem(me + r, devices)
        return (lax.div(other, n_grp), lax.rem(other, n_grp)), other

    barrier = pltpu.get_barrier_semaphore()

    def greet(r, _):
        pl.semaphore_signal(barrier, inc=1, device_id=place(r)[0], device_id_type=MESH)
        return 0

    lax.fori_loop(1, devices, greet, 0)

    wide[...] = jnp.ones_like(wide)
    wide[:, :bands] = pix_ref[...]
    mine[...] = jnp.zeros_like(mine)
    mine[:, :bands] = tgt_ref[...]
    take, put = slot_of(lab_ref[...], slots)
    take_ref[...] = take
    outgoing[...] = dot_n(put, wide[...]).astype(BF16).reshape(devices, group, width)
    pl.semaphore_wait(barrier, devices - 1)

    def ship(src, dst, sends, recvs, r):
        where, other = place(r)
        return pltpu.make_async_remote_copy(
            src_ref=src.at[other], dst_ref=dst.at[me],
            send_sem=sends.at[r], recv_sem=recvs.at[r],
            device_id=where, device_id_type=MESH,
        )

    def lend(r):
        return pltpu.make_async_remote_copy(
            src_ref=mine, dst_ref=library.at[grp],
            send_sem=send_t.at[r], recv_sem=recv_t.at[r],
            device_id=(tile, lax.rem(grp + r, n_grp)), device_id_type=MESH,
        )

    def start_a(r, _):
        ship(outgoing, arrived, send_a, recv_a, r).start()
        return 0

    def wait_a(r, _):
        ship(outgoing, arrived, send_a, recv_a, r).wait()
        return 0

    def start_b(r, _):
        ship(outbound, returned, send_b, recv_b, r).start()
        return 0

    def wait_b(r, _):
        ship(outbound, returned, send_b, recv_b, r).wait()
        return 0

    lax.fori_loop(1, devices, start_a, 0)
    for r in range(1, n_grp):
        lend(r).start()
    arrived[me] = outgoing[me]
    library[grp] = mine[...]
    lax.fori_loop(1, devices, wait_a, 0)

    xf = arrived[...].astype(F32).reshape(devices, owned, CAP, width)
    xs = [xf[:, c].reshape(devices * CAP, width).astype(BF16) for c in range(owned)]
    grams = [cluster_gram(x, bands) for x in xs]
    inverses = invert_all([g[0] for g in grams])
    for r in range(1, n_grp):
        lend(r).wait()
    targets = library[...].reshape(n_grp * mine.shape[0], width)
    tf = targets.astype(F32)
    tnorm = dot_t(jnp.ones((8, width), F32), tf * tf, HI)[0:1]
    res = []
    for x, g, inv in zip(xs, grams, inverses):
        s = cluster_scores(x, targets, tnorm, inv, g[1], g[2], g[3], bands)
        res.append(s.reshape(devices, 1, CAP, s.shape[1]))
    full = jnp.concatenate(res, axis=1).reshape(devices, group, targets.shape[0])
    outbound[...] = full.astype(BF16)
    lax.fori_loop(1, devices, start_b, 0)
    returned[me] = outbound[me]
    lax.fori_loop(1, devices, wait_b, 0)
    out_ref[...] = dot_n(take_ref[...], returned[...].reshape(slots, targets.shape[0])).astype(BF16)


def narrow(pixels, labels, targets):
    n_tile, n_grp = lax.axis_size("tile"), lax.axis_size("grp")
    devices = n_tile * n_grp
    owned = NCLUST // devices
    group = owned * CAP
    rows, bands = pixels.shape
    width = -(-(bands + 1) // LANES) * LANES
    total = targets.shape[0] * n_grp
    vmem = pl.BlockSpec(memory_space=pltpu.VMEM)
    dma = pltpu.SemaphoreType.DMA
    return pl.pallas_call(
        functools.partial(step_body, bands, owned, n_tile, n_grp),
        out_shape=jax.ShapeDtypeStruct((rows, total), BF16),
        in_specs=[vmem] * 3,
        out_specs=vmem,
        scratch_shapes=[
            pltpu.VMEM((rows, width), BF16),
            pltpu.VMEM((devices, group, width), BF16),
            pltpu.VMEM((devices, group, width), BF16),
            pltpu.VMEM((targets.shape[0], width), BF16),
            pltpu.VMEM((n_grp, targets.shape[0], width), BF16),
            pltpu.VMEM((devices, group, total), BF16),
            pltpu.VMEM((devices, group, total), BF16),
            pltpu.VMEM((rows, NCLUST * CAP), BF16),
            dma((devices,)), dma((devices,)),
            dma((n_grp,)), dma((n_grp,)),
            dma((devices,)), dma((devices,)),
        ],
        compiler_params=pltpu.CompilerParams(
            collective_id=0, has_side_effects=True, vmem_limit_bytes=60 * 1024 * 1024
        ),
    )(labels.reshape(1, rows), pixels, targets)


def wide_cluster(pixels, labels, targets):
    n_tile = lax.axis_size("tile")
    n_grp = lax.axis_size("grp")
    band_count = pixels.shape[1]
    per_owner = 2 * NCLUST // n_tile
    target_total = targets.shape[0] * n_grp
    clusters = jnp.arange(NCLUST, dtype=jnp.int32)
    member = (labels[:, None] == clusters[None, :]).astype(jnp.int32)
    local_count = jnp.sum(member, axis=0).astype(jnp.float32)
    counts = lax.psum(local_count, ("tile", "grp"))
    place_rank = jnp.sum(jnp.cumsum(member, axis=0) * member, axis=1) - 1
    owner_pair = labels // per_owner
    inner_slot = labels % per_owner
    slot_width = CAP
    target_tile = 2 * owner_pair
    slot_index = (target_tile * per_owner + inner_slot) * slot_width + place_rank
    slot_total = n_tile * per_owner * slot_width
    outgoing = jnp.zeros((slot_total, band_count), jnp.bfloat16).at[slot_index].set(pixels)
    outgoing = outgoing.reshape(n_tile, per_owner * slot_width, band_count)
    arrived = lax.all_to_all(outgoing, "tile", split_axis=0, concat_axis=0, tiled=True)
    grouped = arrived.reshape(n_tile, per_owner, slot_width, band_count)
    gram_sum = jnp.einsum("scwb,scwd->cbd", grouped, grouped, preferred_element_type=jnp.float32)
    first_sums = jnp.sum(grouped, axis=(0, 2), dtype=jnp.float32)
    gram_sum, first_sums = lax.psum((gram_sum, first_sums), "grp")
    own_pair = lax.axis_index("tile") // 2
    own_counts = lax.dynamic_slice_in_dim(counts, own_pair * per_owner, per_owner, 0)
    own_counts = jnp.maximum(own_counts, 1.0)
    centre = first_sums / own_counts[:, None]
    identity = jnp.eye(band_count, dtype=jnp.float32)
    covariance = (
        gram_sum / own_counts[:, None, None]
        - centre[:, :, None] * centre[:, None, :]
        + 0.05 * identity
    )
    factor = jnp.linalg.cholesky(covariance)
    inverse = jax.scipy.linalg.solve_triangular(
        factor, jnp.broadcast_to(identity, factor.shape), lower=True
    )
    whitened = jnp.einsum(
        "tb,cdb->ctd",
        lax.all_gather(targets, "grp", axis=0, tiled=True).astype(jnp.float32),
        inverse,
        precision=lax.Precision.HIGHEST,
    )
    lib_norm = jnp.sum(whitened * whitened, axis=-1)
    centered = grouped.astype(jnp.float32) - centre[None, :, None, :]
    white_pix = jnp.einsum("scwb,cdb->scwd", centered, inverse, precision=lax.Precision.HIGHEST)
    inner_prod = jnp.einsum("scwd,ctd->scwt", white_pix, whitened, precision=lax.Precision.HIGHEST)
    pix_norm = jnp.sum(white_pix * white_pix, axis=-1)
    result = (
        band_count
        * inner_prod
        * inner_prod
        / ((lib_norm[None, :, None, :] + 1e-06) * (pix_norm[:, :, :, None] + 1e-06))
    )
    outbound = result.astype(jnp.bfloat16).reshape(n_tile, per_owner * slot_width, target_total)
    returned = lax.all_to_all(outbound, "tile", split_axis=0, concat_axis=0, tiled=True)
    flat_scores = returned.reshape(slot_total, target_total)
    return flat_scores[slot_index]


def local(pixels, labels, targets):
    devices = lax.axis_size("tile") * lax.axis_size("grp")
    if NCLUST % devices == 0 and devices * CAP <= pixels.shape[1]:
        return narrow(pixels, labels, targets)
    return wide_cluster(pixels, labels, targets)


def solution(mesh):
    return jax.shard_map(
        local,
        mesh=mesh,
        in_specs=(P(("tile", "grp"), None), P(("tile", "grp")), P("grp", None)),
        out_specs=P(("tile", "grp"), None),
        check_vma=False,
    )
```

```python
import functools

import jax
import jax.numpy as jnp
from jax import lax
from jax.experimental import pallas as pl
from jax.experimental.pallas import tpu as pltpu
from jax.sharding import PartitionSpec as P

NCLUST = 64
CAP = 8
RIDGE = 0.05
LIFT = 1.0
EPS = 1e-06
STEP = 64
LANES = 128
SUB = 8
PIV = 4
MESH = pl.DeviceIdType.MESH
HI = lax.Precision.HIGHEST
F32 = jnp.float32
BF16 = jnp.bfloat16


def dot_t(a, b, prec=None):
    return lax.dot_general(a, b, (((1,), (1,)), ((), ())), precision=prec, preferred_element_type=F32)


def dot_0(a, b, prec=None):
    return lax.dot_general(a, b, (((0,), (0,)), ((), ())), precision=prec, preferred_element_type=F32)


def dot_n(a, b, prec=None):
    return lax.dot_general(a, b, (((1,), (0,)), ((), ())), precision=prec, preferred_element_type=F32)


def halves(v):
    big = v.astype(BF16)
    return big, (v - big.astype(F32)).astype(BF16)


def thirds(v):
    big, rest = v.astype(BF16), v
    rest = rest - big.astype(F32)
    mid = rest.astype(BF16)
    return big, mid, (rest - mid.astype(F32)).astype(BF16)


def outer_update(a, b):
    a1, a2, a3 = thirds(a)
    b1, b2, b3 = thirds(b)
    left = jnp.concatenate([a1, a1, a2, a1, a2, a3], axis=0)
    right = jnp.concatenate([b1, b2, b1, b3, b2, b1], axis=0)
    return dot_0(left, right)


def pivot_inverse(e):
    r = 1.0 / (e[0][0] * e[1][1] - e[0][1] * e[0][1])
    i00, i01, i11 = e[1][1] * r, -e[0][1] * r, e[0][0] * r
    x00 = i00 * e[0][2] + i01 * e[1][2]
    x01 = i00 * e[0][3] + i01 * e[1][3]
    x10 = i01 * e[0][2] + i11 * e[1][2]
    x11 = i01 * e[0][3] + i11 * e[1][3]
    s00 = e[2][2] - (e[0][2] * x00 + e[1][2] * x10)
    s01 = e[2][3] - (e[0][2] * x01 + e[1][2] * x11)
    s11 = e[3][3] - (e[0][3] * x01 + e[1][3] * x11)
    q = 1.0 / (s00 * s11 - s01 * s01)
    t00, t01, t11 = s11 * q, -s01 * q, s00 * q
    y00 = -(x00 * t00 + x01 * t01)
    y01 = -(x00 * t01 + x01 * t11)
    y10 = -(x10 * t00 + x11 * t01)
    y11 = -(x10 * t01 + x11 * t11)
    n00 = i00 - (y00 * x00 + y01 * x01)
    n01 = i01 - (y00 * x10 + y01 * x11)
    n11 = i11 - (y10 * x10 + y11 * x11)
    return [[n00, n01, y00, y01], [n01, n11, y10, y11], [y00, y10, t00, t01], [y01, y11, t01, t11]]


def panel_step(tiles, first, j):
    rows = tiles[0].shape[0]
    at = first + j
    home, off = at // LANES, at % LANES
    group = j // SUB * SUB
    lane8 = lax.broadcasted_iota(jnp.int32, (SUB, LANES), 1)
    lanes = lax.broadcasted_iota(jnp.int32, (rows, LANES), 1)
    sub8 = lax.broadcasted_iota(jnp.int32, (SUB, LANES), 0)
    cols = [jnp.broadcast_to(tiles[home][:, off + c : off + c + 1], (rows, LANES)) for c in range(PIV)]
    spread = lambda v, a: jnp.broadcast_to(v[j + a : j + a + 1, :], (SUB, LANES))
    inv = pivot_inverse([[spread(cols[c], a) for c in range(PIV)] for a in range(PIV)])
    fresh = []
    for t, tile in enumerate(tiles):
        src = [spread(tile, c) for c in range(PIV)]
        kept = tile
        if t == home:
            block = (lane8 >= off) & (lane8 < off + PIV)
            src = [jnp.where(block, jnp.where(lane8 == off + c, 1.0, 0.0), v) for c, v in enumerate(src)]
            kept = jnp.where((lanes >= off) & (lanes < off + PIV), 0.0, tile)
        norm = [(inv[a][0] * src[0] + inv[a][1] * src[1]) + (inv[a][2] * src[2] + inv[a][3] * src[3]) for a in range(PIV)]
        wide = [jnp.concatenate([v] * (rows // SUB), axis=0) for v in norm]
        rest = kept - ((cols[0] * wide[0] + cols[1] * wide[1]) + (cols[2] * wide[2] + cols[3] * wide[3]))
        own = rest[group : group + SUB]
        for a in range(PIV):
            own = jnp.where(sub8 == j - group + a, norm[a], own)
        parts = [rest[:group]] * (group > 0) + [own] + [rest[group + SUB :]] * (group + SUB < rows)
        fresh.append(jnp.concatenate(parts, axis=0) if len(parts) > 1 else parts[0])
    return fresh


def panel_inverse(panels, first):
    rows, width = panels[0].shape
    split = [[p[:, t : t + LANES] for t in range(0, width, LANES)] for p in panels]
    for j in range(0, rows, PIV):
        split = [panel_step(tiles, first, j) for tiles in split]
    return [jnp.concatenate(tiles, axis=1) for tiles in split]


def invert_all(mats, midway):
    size = mats[0].shape[0]
    lane1 = lax.broadcasted_iota(jnp.int32, (1, size), 1)
    for k in range(size // STEP):
        lo = k * STEP
        if k == size // STEP // 2:
            midway()
        inside = (lane1 >= lo) & (lane1 < lo + STEP)
        sign = jnp.where(lane1 < lo, -1.0, jnp.where(inside, 0.0, 1.0))
        rows = [m[lo : lo + STEP, :] for m in mats]
        outs = panel_inverse(rows, lo)
        fresh = []
        for m, r, w in zip(mats, rows, outs):
            kept = jnp.where(inside, 0.0, m)
            upd = kept - outer_update(r * sign, w)
            parts = [upd[:lo]] * (lo > 0) + [w] + [upd[lo + STEP :]] * (lo + STEP < size)
            fresh.append(jnp.concatenate(parts, axis=0))
        mats = fresh
    return mats


def cluster_gram(x, bands):
    size = x.shape[0]
    gram = dot_t(x, x)
    valid = x[:, bands : bands + 1].astype(F32)
    ri = lax.broadcasted_iota(jnp.int32, (size, size), 0)
    ci = lax.broadcasted_iota(jnp.int32, (size, size), 1)
    diag = ri == ci
    valid_row = jnp.sum(jnp.where(diag, valid, 0.0), axis=0, keepdims=True)
    count = jnp.maximum(jnp.sum(valid), 1.0)
    share = 1.0 / count
    mean_r = jnp.sum(gram, axis=0, keepdims=True) * share
    mean_c = jnp.sum(gram, axis=1, keepdims=True) * share
    mean = jnp.sum(mean_r) * share
    mat = (gram - mean_r - mean_c + (mean + LIFT)) * (valid * valid_row) * share
    mat = mat + jnp.where(diag, RIDGE, 0.0)
    return mat, valid, count, diag


def cluster_scores(u, tnorm, inverse, count, diag, bands):
    share = 1.0 / count
    (k1, k2), (u1, u2) = halves(inverse), halves(u)
    z = dot_n(k1, u1) + (dot_n(k1, u2) + dot_n(k2, u1))
    kd = jnp.sum(jnp.where(diag, inverse, 0.0), axis=1, keepdims=True)
    pix = count * (1.0 - RIDGE * kd) - LIFT / (LIFT + RIDGE)
    pix = jnp.maximum(pix, 0.0) + EPS
    lib = (tnorm - jnp.sum(u * z, axis=0, keepdims=True) * share) * (1.0 / RIDGE)
    lib = jnp.maximum(lib, 0.0) + EPS
    return z * z * (bands / pix) * (1.0 / lib)


def slot_of(lab_row, slots):
    count = lab_row.shape[1]
    ri = lax.broadcasted_iota(jnp.int32, (count, count), 0)
    ci = lax.broadcasted_iota(jnp.int32, (count, count), 1)
    lab_row = lab_row.astype(F32)
    lab_col = jnp.sum(jnp.where(ri == ci, lab_row, 0.0), axis=1, keepdims=True)
    same = jnp.where(lab_row == lab_col, 1.0, 0.0)
    rank_col = jnp.sum(jnp.where(ci < ri, same, 0.0), axis=1, keepdims=True)
    rank_row = jnp.sum(jnp.where(ri < ci, same, 0.0), axis=0, keepdims=True)
    idx_col = lab_col * CAP + rank_col
    idx_row = lab_row * CAP + rank_row
    across = lax.broadcasted_iota(jnp.int32, (count, slots), 1).astype(F32)
    down = lax.broadcasted_iota(jnp.int32, (slots, count), 0).astype(F32)
    take = jnp.where(across == idx_col, 1.0, 0.0).astype(BF16)
    put = jnp.where(down == idx_row, 1.0, 0.0).astype(BF16)
    return take, put


def step_body(
    bands, owned, n_tile, n_grp,
    lab_ref, pix_ref, tgt_ref, out_ref,
    wide, outgoing, arrived, mine, library, outbound, returned, take_ref,
    send_a, recv_a, send_t, recv_t, send_b, recv_b,
):
    devices = n_tile * n_grp
    group = owned * CAP
    slots = devices * group
    width = wide.shape[1]
    total = outbound.shape[2]
    tile = lax.axis_index("tile")
    grp = lax.axis_index("grp")
    me = tile * n_grp + grp

    def place(r):
        other = lax.rem(me + r, devices)
        return (lax.div(other, n_grp), lax.rem(other, n_grp)), other

    barrier = pltpu.get_barrier_semaphore()

    def greet(r, _):
        pl.semaphore_signal(barrier, inc=1, device_id=place(r)[0], device_id_type=MESH)
        return 0

    lax.fori_loop(1, devices, greet, 0)

    wide[...] = jnp.ones_like(wide)
    wide[:, :bands] = pix_ref[...]
    mine[...] = jnp.zeros_like(mine)
    mine[:, :bands] = tgt_ref[...]
    take, put = slot_of(lab_ref[...], slots)
    take_ref[...] = take
    outgoing[...] = dot_n(put, wide[...]).astype(BF16).reshape(devices, group, width)
    pl.semaphore_wait(barrier, devices - 1)

    def ship(src, dst, sends, recvs, r):
        where, other = place(r)
        return pltpu.make_async_remote_copy(
            src_ref=src.at[other], dst_ref=dst.at[me],
            send_sem=sends.at[r], recv_sem=recvs.at[r],
            device_id=where, device_id_type=MESH,
        )

    def lend(r):
        return pltpu.make_async_remote_copy(
            src_ref=mine, dst_ref=library.at[grp],
            send_sem=send_t.at[r], recv_sem=recv_t.at[r],
            device_id=(tile, lax.rem(grp + r, n_grp)), device_id_type=MESH,
        )

    def start_a(r, _):
        ship(outgoing, arrived, send_a, recv_a, r).start()
        return 0

    def wait_a(r, _):
        ship(outgoing, arrived, send_a, recv_a, r).wait()
        return 0

    def start_b(r, _):
        ship(outbound, returned, send_b, recv_b, r).start()
        return 0

    def wait_b(r, _):
        ship(outbound, returned, send_b, recv_b, r).wait()
        return 0

    lax.fori_loop(1, devices, start_a, 0)
    for r in range(1, n_grp):
        lend(r).start()
    arrived[me] = outgoing[me]
    library[grp] = mine[...]
    lax.fori_loop(1, devices, wait_a, 0)

    xf = arrived[...].astype(F32).reshape(devices, owned, CAP, width)
    xs = [xf[:, c].reshape(devices * CAP, width).astype(BF16) for c in range(owned)]
    grams = [cluster_gram(x, bands) for x in xs]
    held = {}

    def midway():
        for r in range(1, n_grp):
            lend(r).wait()
        targets = library[...].reshape(n_grp * mine.shape[0], width)
        tf = targets.astype(F32)
        held["norm"] = dot_t(jnp.ones((8, width), F32), tf * tf, HI)[0:1]
        for c, (x, g) in enumerate(zip(xs, grams)):
            u = dot_t(x, targets)
            held[c] = (u - jnp.sum(u, axis=0, keepdims=True) * (1.0 / g[2])) * g[1]

    inverses = invert_all([g[0] for g in grams], midway)
    res = []
    for c, (g, inv) in enumerate(zip(grams, inverses)):
        s = cluster_scores(held[c], held["norm"], inv, g[2], g[3], bands)
        res.append(s.reshape(devices, 1, CAP, s.shape[1]))
    full = jnp.concatenate(res, axis=1).reshape(devices, group, total)
    outbound[...] = full.astype(BF16)
    lax.fori_loop(1, devices, start_b, 0)
    returned[me] = outbound[me]
    lax.fori_loop(1, devices, wait_b, 0)
    out_ref[...] = dot_n(take_ref[...], returned[...].reshape(slots, total)).astype(BF16)


def narrow(pixels, labels, targets):
    n_tile, n_grp = lax.axis_size("tile"), lax.axis_size("grp")
    devices = n_tile * n_grp
    owned = NCLUST // devices
    group = owned * CAP
    rows, bands = pixels.shape
    width = -(-(bands + 1) // LANES) * LANES
    total = targets.shape[0] * n_grp
    vmem = pl.BlockSpec(memory_space=pltpu.VMEM)
    dma = pltpu.SemaphoreType.DMA
    return pl.pallas_call(
        functools.partial(step_body, bands, owned, n_tile, n_grp),
        out_shape=jax.ShapeDtypeStruct((rows, total), BF16),
        in_specs=[vmem] * 3,
        out_specs=vmem,
        scratch_shapes=[
            pltpu.VMEM((rows, width), BF16),
            pltpu.VMEM((devices, group, width), BF16),
            pltpu.VMEM((devices, group, width), BF16),
            pltpu.VMEM((targets.shape[0], width), BF16),
            pltpu.VMEM((n_grp, targets.shape[0], width), BF16),
            pltpu.VMEM((devices, group, total), BF16),
            pltpu.VMEM((devices, group, total), BF16),
            pltpu.VMEM((rows, NCLUST * CAP), BF16),
            dma((devices,)), dma((devices,)),
            dma((n_grp,)), dma((n_grp,)),
            dma((devices,)), dma((devices,)),
        ],
        compiler_params=pltpu.CompilerParams(
            collective_id=0, has_side_effects=True, vmem_limit_bytes=60 * 1024 * 1024
        ),
    )(labels.reshape(1, rows), pixels, targets)


def wide_cluster(pixels, labels, targets):
    n_tile = lax.axis_size("tile")
    n_grp = lax.axis_size("grp")
    band_count = pixels.shape[1]
    per_owner = 2 * NCLUST // n_tile
    target_total = targets.shape[0] * n_grp
    clusters = jnp.arange(NCLUST, dtype=jnp.int32)
    member = (labels[:, None] == clusters[None, :]).astype(jnp.int32)
    local_count = jnp.sum(member, axis=0).astype(jnp.float32)
    counts = lax.psum(local_count, ("tile", "grp"))
    place_rank = jnp.sum(jnp.cumsum(member, axis=0) * member, axis=1) - 1
    owner_pair = labels // per_owner
    inner_slot = labels % per_owner
    slot_width = CAP
    target_tile = 2 * owner_pair
    slot_index = (target_tile * per_owner + inner_slot) * slot_width + place_rank
    slot_total = n_tile * per_owner * slot_width
    outgoing = jnp.zeros((slot_total, band_count), jnp.bfloat16).at[slot_index].set(pixels)
    outgoing = outgoing.reshape(n_tile, per_owner * slot_width, band_count)
    arrived = lax.all_to_all(outgoing, "tile", split_axis=0, concat_axis=0, tiled=True)
    grouped = arrived.reshape(n_tile, per_owner, slot_width, band_count)
    gram_sum = jnp.einsum("scwb,scwd->cbd", grouped, grouped, preferred_element_type=jnp.float32)
    first_sums = jnp.sum(grouped, axis=(0, 2), dtype=jnp.float32)
    gram_sum, first_sums = lax.psum((gram_sum, first_sums), "grp")
    own_pair = lax.axis_index("tile") // 2
    own_counts = lax.dynamic_slice_in_dim(counts, own_pair * per_owner, per_owner, 0)
    own_counts = jnp.maximum(own_counts, 1.0)
    centre = first_sums / own_counts[:, None]
    identity = jnp.eye(band_count, dtype=jnp.float32)
    covariance = (
        gram_sum / own_counts[:, None, None]
        - centre[:, :, None] * centre[:, None, :]
        + 0.05 * identity
    )
    factor = jnp.linalg.cholesky(covariance)
    inverse = jax.scipy.linalg.solve_triangular(
        factor, jnp.broadcast_to(identity, factor.shape), lower=True
    )
    whitened = jnp.einsum(
        "tb,cdb->ctd",
        lax.all_gather(targets, "grp", axis=0, tiled=True).astype(jnp.float32),
        inverse,
        precision=lax.Precision.HIGHEST,
    )
    lib_norm = jnp.sum(whitened * whitened, axis=-1)
    centered = grouped.astype(jnp.float32) - centre[None, :, None, :]
    white_pix = jnp.einsum("scwb,cdb->scwd", centered, inverse, precision=lax.Precision.HIGHEST)
    inner_prod = jnp.einsum("scwd,ctd->scwt", white_pix, whitened, precision=lax.Precision.HIGHEST)
    pix_norm = jnp.sum(white_pix * white_pix, axis=-1)
    result = (
        band_count
        * inner_prod
        * inner_prod
        / ((lib_norm[None, :, None, :] + 1e-06) * (pix_norm[:, :, :, None] + 1e-06))
    )
    outbound = result.astype(jnp.bfloat16).reshape(n_tile, per_owner * slot_width, target_total)
    returned = lax.all_to_all(outbound, "tile", split_axis=0, concat_axis=0, tiled=True)
    flat_scores = returned.reshape(slot_total, target_total)
    return flat_scores[slot_index]


def local(pixels, labels, targets):
    devices = lax.axis_size("tile") * lax.axis_size("grp")
    if NCLUST % devices == 0 and devices * CAP <= pixels.shape[1]:
        return narrow(pixels, labels, targets)
    return wide_cluster(pixels, labels, targets)


def solution(mesh):
    return jax.shard_map(
        local,
        mesh=mesh,
        in_specs=(P(("tile", "grp"), None), P(("tile", "grp")), P("grp", None)),
        out_specs=P(("tile", "grp"), None),
        check_vma=False,
    )
```
